512 devices in a mesh: seq: 64 (over y_hi, z, core), tp: 8 (over x, y_lo).
Axes of the slice: x: 4, y: 8 (y_hi: 4, y_lo: 2; y = y_hi * 2 + y_lo), z: 8, core: 2. Of those that a mesh axis runs over, the one named last changes fastest.
Arguments:
- resid: bfloat16 [8192, 2048], P('seq'), may hold values from -1.5 to 1.5
- query: bfloat16 [8192, 1024], P('seq', 'tp'), may hold values from -6 to 6
- key_new: bfloat16 [8192, 1024], P('seq', 'tp'), may hold values from -6 to 6
- value_new: bfloat16 [8192, 1024], P('seq', 'tp'), may hold values from -6 to 6
- key_cache: bfloat16 [1024, 1024], P('seq', 'tp'), may hold values from -6 to 6
- value_cache: bfloat16 [1024, 1024], P('seq', 'tp'), may hold values from -6 to 6
- cache_len: int32 [64], replicated, may hold values from 0 to 16, as said below
- out_weight: bfloat16 [1024, 2048], P('tp'), may hold values from -0.1875 to 0.1875
- norm_gain: bfloat16 [2048], replicated, may hold values from 0.099609375 to 1.8984375
- router: bfloat16 [2048, 64], replicated, may hold values from -2 to 2
- expert_ids: int32 [8192, 6], P('seq'), may hold values from 0 to 63, all different within a row; in each aligned block of 128 rows (0 to 127, 128 to 255, ...) at most 18 rows name the same one
- w_gate: bfloat16 [64, 2048, 1408], P('seq', None, 'tp'), may hold values from -0.125 to 0.125
- w_up: bfloat16 [64, 2048, 1408], P('seq', None, 'tp'), may hold values from -0.125 to 0.125
- w_down: bfloat16 [64, 1408, 2048], P('seq', None, 'tp'), may hold values from -0.15625 to 0.15625
- w_shared_gate: bfloat16 [2048, 1408], P('seq', 'tp'), may hold values from -0.125 to 0.125
- w_shared_up: bfloat16 [2048, 1408], P('seq', 'tp'), may hold values from -0.125 to 0.125
- w_shared_down: bfloat16 [1408, 2048], P('tp', 'seq'), may hold values from -0.15625 to 0.15625
Outputs:
- mixed: bfloat16 [8192, 2048], P('seq', 'tp')
The draws below stay inside these ranges and needn't reach their ends.
Inputs may be any that keep to these rules, and one draw needn't show every extreme that they name: `cache_len`: some cache block has all 16 rows valid and another has none. `expert_ids`: each row names 6 different experts; the rows of one device name no expert more than 18 times, a bound that some block reaches.
All inputs are finite; a program needn't handle non-finite values.
Results may differ from the reference program's by a relative error of at most 0.013.
Values may be sent and summed in bfloat16 or wider, within the bound.
No kernel may reach another device: no remote copies, remote signals or barrier semaphores. Data moves between devices by JAX's collectives and lax.ppermute only.
A program may use at most 64 MiB of HBM per device.

```python
import math
import jax
import jax.numpy as jnp
import numpy as np
from jax import lax

D = 2048
HEADS = 8
HD = 128
FF = 1408
SHARED_FF = 1408
TOPK = 6
TOK_DEV = 128
CBLK = 16
EXPERTS = 64
CAP = 18
CACHE = 1024
TOKENS = 8192
N_SEQ = 64


def draw_query(key, part):
    base = jnp.clip(2.0 * jax.random.normal(jax.random.fold_in(key, 1), (TOKENS, HEADS * HD), jnp.float32), -6.0, 6.0)
    return base.astype(jnp.bfloat16)


def draw_key_new(key, part):
    base = jnp.clip(jax.random.normal(jax.random.fold_in(key, 2), (TOKENS, HEADS * HD), jnp.float32), -6.0, 6.0)
    return base.astype(jnp.bfloat16)


def draw_router(key, part):
    base = jnp.clip(2.0 / math.sqrt(D) * jax.random.normal(jax.random.fold_in(key, 3), (D, EXPERTS), jnp.float32), -0.5, 0.5)
    return base.astype(jnp.bfloat16)


def draw_cache_len(key, part):
    lengths = jax.random.randint(jax.random.fold_in(key, 4), (N_SEQ,), 0, CBLK + 1)
    order = jax.random.permutation(jax.random.fold_in(key, 5), N_SEQ)
    lengths = lengths.at[order[0]].set(CBLK)
    lengths = lengths.at[order[1]].set(0)
    return lengths.astype(jnp.int32)


def block_levels(own_key, shape, cuts, least, high):
    gain = 1.0
    for position, shards_of in cuts:
        draws = jax.random.uniform(jax.random.fold_in(jax.random.fold_in(own_key, 6), position), (shards_of,), jnp.float32, least / len(cuts), high / len(cuts))
        gain = gain * jnp.repeat(jnp.exp(draws), shape[position] // shards_of).reshape((-1,) + (1,) * (len(shape) - 1 - position))
    return gain


def routed_block(rng, own, number, rows, amount, top, bound, lean):
    sequence = jax.random.permutation(rng, amount)
    packed, ordinary = load_shares(amount, rows * top, bound, lean, True), load_shares(amount, rows * top, bound, lean, False)
    places = jnp.arange(amount)

    def named(tallies, offset_by):
        used = int((tallies > 0).sum())
        fixed = max(1, used // 4)
        passed = fixed + (places - fixed + offset_by * (used - fixed)) % max(1, amount - fixed)
        return jnp.zeros((amount,), jnp.int32).at[sequence[jnp.where(places < fixed, places, passed)]].set(jnp.asarray(tallies, jnp.int32))

    tallies = jnp.where(number % 4 == 0, named(packed, number // 4), named(ordinary, number - number // 4 - 1))
    mixed = jax.random.permutation(jax.random.fold_in(own, 3), amount)
    giver, sink = mixed[0:amount // 2 * 2:2], mixed[1:amount // 2 * 2:2]
    slack = jnp.minimum(tallies[giver] - 1, bound - tallies[sink]) // 2
    slack = jnp.where((giver == sequence[0]) | (sink == sequence[0]) | (tallies[sink] == 0), 0, jnp.maximum(slack, 0))
    passed = jax.random.randint(jax.random.fold_in(own, 4), (amount // 2,), 0, 1 << 20) % (slack + 1)
    tallies = tallies.at[giver].add(-passed).at[sink].add(passed)
    labels = jnp.searchsorted(jnp.cumsum(tallies), jnp.arange(rows * top), side="right").astype(jnp.int32)
    listing = labels.reshape(top, rows).T
    listing = listing[jax.random.permutation(jax.random.fold_in(own, 1), rows)]
    offset_by = jax.random.randint(jax.random.fold_in(own, 2), (rows, 1), 0, top)
    return jnp.take_along_axis(listing, (jnp.arange(top)[None, :] + offset_by) % top, axis=1)


def load_shares(number_of, total, limit, skew, full):
    portions = [(1 << 20) // math.isqrt(standing ** skew) + 1 for standing in range(1, number_of + 1)]
    largest = limit if full else min(limit, max(-(-total // number_of), total * portions[0] // sum(portions)))
    least = 1 if total - largest >= number_of - 1 else 0
    given, surplus = [largest] + [least] * (number_of - 1), total - largest - least * (number_of - 1)
    while surplus > 0:
        free = [i for i in range(1, number_of) if given[i] < largest] or [i for i in range(1, number_of) if given[i] < limit]
        pool, left = sum([portions[i] for i in free]), surplus
        for i in free:
            addition = min(limit - given[i], max(1, left * portions[i] // pool), surplus)
            given[i] = given[i] + addition
            surplus = surplus - addition
    return np.array(given)


def noise(rng, dims, scale, bound, split=(), held_as=jnp.bfloat16):
    level = block_levels(rng, dims, split, -0.22, 0.18) if split else 1.0
    entries = jax.random.normal(rng, dims, jnp.float32) * scale * level
    return jnp.minimum(jnp.maximum(entries, -bound), bound).astype(held_as)


def setup_inputs(seed: int = 0) -> dict:
    key_of = jax.random.split(jax.random.key(seed), 18)
    resid = noise(key_of[0], (TOKENS, D), 0.25, 1.5, ((0, 64),))
    query = draw_query(jax.random.fold_in(key_of[17], 71), 0)
    key_new = draw_key_new(jax.random.fold_in(key_of[17], 71), 0)
    value_new = noise(key_of[3], (TOKENS, HEADS * HD), 1.0, 6.0, ((0, 64), (1, 8)))
    key_cache = noise(key_of[4], (CACHE, HEADS * HD), 1.0, 6.0, ((0, 64), (1, 8)))
    value_cache = noise(key_of[5], (CACHE, HEADS * HD), 1.0, 6.0, ((0, 64), (1, 8)))
    cache_len = draw_cache_len(jax.random.fold_in(key_of[17], 71), 0)
    out_weight = noise(key_of[7], (HEADS * HD, D), (HEADS * HD) ** -0.5, 0.1875, ((0, 8),))
    norm_gain = jnp.clip(1.0 + 0.18 * jax.random.normal(key_of[8], (D,), jnp.float32), 0.099609375, 1.8984375).astype(jnp.bfloat16)
    router = draw_router(jax.random.fold_in(key_of[17], 71), 0)
    expert_ids_keys = jax.random.split(jax.random.fold_in(key_of[10], 1), TOKENS // TOK_DEV)
    expert_ids_turns = jax.random.permutation(jax.random.fold_in(key_of[10], 3), TOKENS // TOK_DEV)
    expert_ids = jax.vmap(lambda own, number: routed_block(jax.random.fold_in(key_of[10], 2), own, number, TOK_DEV, EXPERTS, TOPK, CAP, 2))(expert_ids_keys, expert_ids_turns).reshape((TOKENS, TOPK))
    w_gate = noise(key_of[11], (EXPERTS, D, FF), D ** -0.5, 0.125, ((0, 64), (2, 8)))
    w_up = noise(key_of[12], (EXPERTS, D, FF), D ** -0.5, 0.125, ((0, 64), (2, 8)))
    w_down = noise(key_of[13], (EXPERTS, FF, D), FF ** -0.5, 0.15625, ((0, 64), (2, 8)))
    w_shared_gate = noise(key_of[14], (D, SHARED_FF), D ** -0.5, 0.125, ((0, 64), (1, 8)))
    w_shared_up = noise(key_of[15], (D, SHARED_FF), D ** -0.5, 0.125, ((0, 64), (1, 8)))
    w_shared_down = noise(key_of[16], (SHARED_FF, D), SHARED_FF ** -0.5, 0.15625, ((0, 8), (1, 64)))
    return dict(resid=resid, query=query, key_new=key_new, value_new=value_new, key_cache=key_cache, value_cache=value_cache, cache_len=cache_len, out_weight=out_weight, norm_gain=norm_gain, router=router, expert_ids=expert_ids, w_gate=w_gate, w_up=w_up, w_down=w_down, w_shared_gate=w_shared_gate, w_shared_up=w_shared_up, w_shared_down=w_shared_down)


def reference(resid, query, key_new, value_new, key_cache, value_cache, cache_len, out_weight, norm_gain, router, expert_ids, w_gate, w_up, w_down, w_shared_gate, w_shared_up, w_shared_down):
    all_keys = jnp.concatenate([key_cache, key_new], 0).reshape(CACHE + TOKENS, HEADS, HD).transpose(1, 0, 2)
    all_values = jnp.concatenate([value_cache, value_new], 0).reshape(CACHE + TOKENS, HEADS, HD).transpose(1, 0, 2)
    queries = query.reshape(TOKENS, HEADS, HD).transpose(1, 0, 2)
    cache_open = (jnp.arange(CBLK, dtype=jnp.int32)[None, :] < cache_len[:, None]).reshape(CACHE)
    fresh_open = jnp.arange(TOKENS)[None, :] <= jnp.arange(TOKENS)[:, None]
    visible = jnp.concatenate([jnp.broadcast_to(cache_open[None, :], (TOKENS, CACHE)), fresh_open], 1)

    def one_head(items):
        q_rows, k_rows, v_rows = items
        scores = jnp.dot(q_rows.astype(jnp.float32), k_rows.astype(jnp.float32).T) / math.sqrt(HD)
        scores = jnp.where(visible, scores, -jnp.inf)
        top_score = lax.optimization_barrier(jnp.max(scores, axis=-1, keepdims=True))
        weights = jnp.exp(scores - top_score)
        probs = (weights / lax.optimization_barrier(jnp.sum(weights, axis=-1, keepdims=True))).astype(jnp.bfloat16)
        return jnp.dot(probs.astype(jnp.float32), v_rows.astype(jnp.float32)).astype(jnp.bfloat16)
    attn = lax.map(one_head, (queries, all_keys, all_values))
    attn = attn.transpose(1, 0, 2).reshape(TOKENS, HEADS * HD)
    hidden_state = resid.astype(jnp.float32) + jnp.dot(attn, out_weight, preferred_element_type=jnp.float32)
    mean_square = lax.optimization_barrier(jnp.mean(hidden_state * hidden_state, axis=-1, keepdims=True))
    normed = (hidden_state * lax.rsqrt(mean_square + 1e-06) * norm_gain.astype(jnp.float32)).astype(jnp.bfloat16)
    logits = jnp.dot(normed, router, preferred_element_type=jnp.float32)
    picked = jnp.take_along_axis(logits, expert_ids, axis=1)
    gates = jax.nn.softmax(picked, axis=-1)
    shared_gate = jnp.dot(normed, w_shared_gate, preferred_element_type=jnp.float32)
    shared_up = jnp.dot(normed, w_shared_up, preferred_element_type=jnp.float32)
    shared_inner = (jax.nn.silu(shared_gate) * shared_up).astype(jnp.bfloat16)
    shared_out = jnp.dot(shared_inner, w_shared_down, preferred_element_type=jnp.float32)
    block_ids = expert_ids.reshape(N_SEQ, TOK_DEV * TOPK)
    one_hot = (block_ids[:, :, None] == jnp.arange(EXPERTS, dtype=jnp.int32)[None, None, :]).astype(jnp.int32)
    before = jnp.cumsum(one_hot, axis=1) - one_hot
    slot = lax.optimization_barrier(jnp.sum(one_hot * before, axis=-1)).astype(jnp.int32)
    device_of = jnp.broadcast_to(jnp.arange(N_SEQ, dtype=jnp.int32)[:, None], (N_SEQ, TOK_DEV * TOPK))
    token_of = jnp.repeat(jnp.arange(TOKENS, dtype=jnp.int32), TOPK).reshape(N_SEQ, TOK_DEV * TOPK)
    source = jnp.full((EXPERTS, N_SEQ, CAP), TOKENS, jnp.int32).at[block_ids, device_of, slot].set(token_of)
    normed_pad = jnp.concatenate([normed, jnp.zeros((1, D), jnp.bfloat16)], 0)

    def run_expert(items):
        gate_w, up_w, down_w, rows_of = items
        rows = normed_pad[rows_of.reshape(-1)]
        gate_pre = jnp.dot(rows, gate_w, preferred_element_type=jnp.float32)
        up_pre = jnp.dot(rows, up_w, preferred_element_type=jnp.float32)
        inner = (jax.nn.silu(gate_pre) * up_pre).astype(jnp.bfloat16)
        return jnp.dot(inner, down_w, preferred_element_type=jnp.float32).astype(jnp.bfloat16)
    expert_out = lax.map(run_expert, (w_gate, w_up, w_down, source))
    flat_out = expert_out.reshape(EXPERTS * N_SEQ * CAP, D)
    where_row = (block_ids * (N_SEQ * CAP) + device_of * CAP + slot).reshape(TOKENS, TOPK)
    total = hidden_state + shared_out
    for which in range(TOPK):
        total = total + gates[:, which:which + 1] * flat_out[where_row[:, which]].astype(jnp.float32)
    return total.astype(jnp.bfloat16)
```

```python
import math

import jax
import jax.numpy as jnp
import numpy as np
from jax import lax
from jax.sharding import Mesh
from jax.sharding import PartitionSpec as P

D = 2048
HD = 128
TOPK = 6
CAP = 18

SEQ = ("yh", "z", "c")
TP = ("x", "yl")


def gather_seq(x):
    g = lax.all_gather(x, "yh", axis=0)
    g = lax.all_gather(g, "z", axis=0)
    g = lax.all_gather(g, "c", axis=0)
    return g


def local(
    resid,
    query,
    key_new,
    value_new,
    key_cache,
    value_cache,
    cache_len,
    out_weight,
    norm_gain,
    router,
    expert_ids,
    w_gate,
    w_up,
    w_down,
    w_shared_gate,
    w_shared_up,
    w_shared_down,
):
    tok_rows = query.shape[0]
    block_rows = key_cache.shape[0]
    n_yh, n_z, n_c = (lax.axis_size(a) for a in SEQ)
    n_x, n_yl = (lax.axis_size(a) for a in TP)
    n_seq = n_yh * n_z * n_c
    n_tp = n_x * n_yl
    seq_index = (lax.axis_index("yh") * n_z + lax.axis_index("z")) * n_c + lax.axis_index("c")
    tp_index = lax.axis_index("x") * n_yl + lax.axis_index("yl")
    width = D // n_tp

    ow_all = lax.all_gather(out_weight, TP, axis=0)
    wpack = jnp.stack([w_shared_gate, w_shared_up, w_shared_down.T], 0)
    wg = gather_seq(wpack)
    wg = jnp.transpose(wg, (2, 1, 0, 3, 4, 5)).reshape(n_seq, 3, wpack.shape[1], wpack.shape[2])
    sg_w = wg[:, 0].reshape(n_seq * wpack.shape[1], wpack.shape[2])
    su_w = wg[:, 1].reshape(n_seq * wpack.shape[1], wpack.shape[2])
    sd_t = wg[:, 2].reshape(n_tp, n_seq // n_tp, wpack.shape[1], wpack.shape[2])
    sd_own = lax.all_to_all(sd_t, TP, split_axis=0, concat_axis=0, tiled=True)

    kv = jnp.concatenate([key_cache, key_new, value_cache, value_new], 0)
    kvg = gather_seq(kv).reshape(n_seq, kv.shape[0], HD)
    pos = jnp.arange(n_seq, dtype=jnp.int32)
    src = (pos % n_yh) * (n_z * n_c) + ((pos // n_yh) % n_z) * n_c + pos // (n_yh * n_z)
    ck = kvg[:, :block_rows].reshape(n_seq * block_rows, HD)
    nk = kvg[:, block_rows:block_rows + tok_rows].reshape(n_seq * tok_rows, HD)
    cv = kvg[:, block_rows + tok_rows:2 * block_rows + tok_rows].reshape(n_seq * block_rows, HD)
    nv = kvg[:, 2 * block_rows + tok_rows:].reshape(n_seq * tok_rows, HD)

    scale = 1.0 / math.sqrt(HD)
    s_c = jnp.dot(query, ck.T, preferred_element_type=jnp.float32) * scale
    s_n = jnp.dot(query, nk.T, preferred_element_type=jnp.float32) * scale
    c_open = (
        jnp.arange(block_rows, dtype=jnp.int32)[None, :] < cache_len[src][:, None]
    ).reshape(n_seq * block_rows)
    key_place = (src[:, None] * tok_rows + jnp.arange(tok_rows, dtype=jnp.int32)[None, :]).reshape(
        n_seq * tok_rows
    )
    query_place = seq_index * tok_rows + jnp.arange(tok_rows, dtype=jnp.int32)
    n_open = key_place[None, :] <= query_place[:, None]
    s_c = jnp.where(c_open[None, :], s_c, -jnp.inf)
    s_n = jnp.where(n_open, s_n, -jnp.inf)
    top = jnp.maximum(jnp.max(s_c, axis=-1, keepdims=True), jnp.max(s_n, axis=-1, keepdims=True))
    e_c = jnp.exp(s_c - top)
    e_n = jnp.exp(s_n - top)
    total = jnp.sum(e_c, axis=-1, keepdims=True) + jnp.sum(e_n, axis=-1, keepdims=True)
    p_c = (e_c / total).astype(jnp.bfloat16)
    p_n = (e_n / total).astype(jnp.bfloat16)
    attn = jnp.dot(p_c, cv, preferred_element_type=jnp.float32) + jnp.dot(
        p_n, nv, preferred_element_type=jnp.float32
    )
    attn = attn.astype(jnp.bfloat16)

    attn_all = lax.all_gather(attn, TP, axis=0)
    hidden_state = resid.astype(jnp.float32) + jnp.einsum(
        "tqd,tdn->qn", attn_all, ow_all, preferred_element_type=jnp.float32
    )
    mean_square = jnp.mean(hidden_state * hidden_state, axis=-1, keepdims=True)
    normed = (hidden_state * lax.rsqrt(mean_square + 1e-06) * norm_gain.astype(jnp.float32)).astype(
        jnp.bfloat16
    )
    own_hidden = lax.dynamic_slice_in_dim(hidden_state, tp_index * width, width, 1)
    own_normed = lax.dynamic_slice_in_dim(normed, tp_index * width, width, 1)

    logits = jnp.dot(normed, router, preferred_element_type=jnp.float32)
    expert_count = router.shape[1]
    expert_range = jnp.arange(expert_count, dtype=jnp.int32)
    picked = jnp.sum(
        jnp.where(expert_ids[:, :, None] == expert_range[None, None, :], logits[:, None, :], 0.0),
        axis=-1,
    )
    gates = jax.nn.softmax(picked, axis=-1)

    shared_gate = jnp.dot(normed, sg_w, preferred_element_type=jnp.float32)
    shared_up = jnp.dot(normed, su_w, preferred_element_type=jnp.float32)
    shared_inner = (jax.nn.silu(shared_gate) * shared_up).astype(jnp.bfloat16)
    inner_all = lax.all_gather(shared_inner, TP, axis=0)
    shared_own = jnp.einsum(
        "tqf,tsjf->qsj", inner_all, sd_own, preferred_element_type=jnp.float32
    ).reshape(tok_rows, width)

    flat_ids = expert_ids.reshape(tok_rows * TOPK)
    one_hot = (flat_ids[:, None] == expert_range[None, :]).astype(jnp.int32)
    before = jnp.cumsum(one_hot, axis=0) - one_hot
    slot = jnp.sum(one_hot * before, axis=1)
    dest = flat_ids * CAP + slot
    slots = expert_count * CAP
    place = (dest[None, :] == jnp.arange(slots, dtype=jnp.int32)[:, None]).reshape(
        slots, tok_rows, TOPK
    )
    dispatch = jnp.any(place, axis=-1).astype(jnp.bfloat16)
    buffer = jnp.dot(dispatch, own_normed, preferred_element_type=jnp.float32).astype(jnp.bfloat16)
    buffer = buffer.reshape(expert_count, CAP, width)
    recv = lax.all_to_all(buffer, SEQ, split_axis=0, concat_axis=0, tiled=True)
    rows_all = lax.all_gather(recv, TP, axis=0)
    ff = w_gate.shape[2]
    gate_pre = jnp.einsum(
        "tsrc,tcf->srf", rows_all, w_gate[0].reshape(n_tp, width, ff), preferred_element_type=jnp.float32
    )
    up_pre = jnp.einsum(
        "tsrc,tcf->srf", rows_all, w_up[0].reshape(n_tp, width, ff), preferred_element_type=jnp.float32
    )
    inner = (jax.nn.silu(gate_pre) * up_pre).astype(jnp.bfloat16)
    inner_r = lax.all_gather(inner, TP, axis=0)
    out = jnp.einsum(
        "tsrf,tfn->srn",
        inner_r,
        w_down[0].reshape(n_tp, ff, w_down.shape[2]),
        preferred_element_type=jnp.float32,
    ).astype(jnp.bfloat16)
    returned = lax.all_to_all(out, SEQ, split_axis=0, concat_axis=0, tiled=True)
    picked_rows = returned.reshape(slots, width)[dest]
    weighted = picked_rows.astype(jnp.float32) * gates.reshape(tok_rows * TOPK)[:, None]
    routed = jnp.sum(weighted.reshape(tok_rows, TOPK, width), axis=1)
    return (own_hidden + shared_own + routed).astype(jnp.bfloat16)


def solution(mesh):
    n_seq, n_tp = mesh.devices.shape
    fine = Mesh(mesh.devices.reshape(n_seq // 16, 8, 2, n_tp // 2, 2), SEQ + TP)
    return jax.shard_map(
        local,
        mesh=fine,
        in_specs=(
            P(SEQ, None),
            P(SEQ, TP),
            P(SEQ, TP),
            P(SEQ, TP),
            P(SEQ, TP),
            P(SEQ, TP),
            P(),
            P(TP, None),
            P(),
            P(),
            P(SEQ, None),
            P(SEQ, None, TP),
            P(SEQ, None, TP),
            P(SEQ, None, TP),
            P(SEQ, TP),
            P(SEQ, TP),
            P(TP, SEQ),
        ),
        out_specs=P(SEQ, TP),
        check_vma=False,
    )
```

```python
import math

import jax
import jax.numpy as jnp
import numpy as np
from jax import lax
from jax.sharding import Mesh
from jax.sharding import PartitionSpec as P

D = 2048
HD = 128
TOPK = 6
CAP = 18

SEQ = ("yh", "z", "c")
TP = ("x", "yl")


def gather_seq(x):
    g = lax.all_gather(x, "yh", axis=0)
    g = lax.all_gather(g, "z", axis=0)
    g = lax.all_gather(g, "c", axis=0)
    return g


def tp_blocks(x, n_tp):
    out = [x]
    for k in range(1, n_tp):
        out.append(lax.ppermute(x, TP, [(j, (j + k) % n_tp) for j in range(n_tp)]))
    return out


def local(
    resid,
    query,
    key_new,
    value_new,
    key_cache,
    value_cache,
    cache_len,
    out_weight,
    norm_gain,
    router,
    expert_ids,
    w_gate,
    w_up,
    w_down,
    w_shared_gate,
    w_shared_up,
    w_shared_down,
):
    tok_rows = query.shape[0]
    block_rows = key_cache.shape[0]
    n_yh, n_z, n_c = (lax.axis_size(a) for a in SEQ)
    n_x, n_yl = (lax.axis_size(a) for a in TP)
    n_seq = n_yh * n_z * n_c
    n_tp = n_x * n_yl
    seq_index = (lax.axis_index("yh") * n_z + lax.axis_index("z")) * n_c + lax.axis_index("c")
    tp_index = lax.axis_index("x") * n_yl + lax.axis_index("yl")
    width = D // n_tp

    ow_blocks = tp_blocks(out_weight, n_tp)
    wpack = jnp.stack([w_shared_gate, w_shared_up, w_shared_down.T], 0)
    wg = gather_seq(wpack)
    wg = jnp.transpose(wg, (2, 1, 0, 3, 4, 5)).reshape(n_seq, 3, wpack.shape[1], wpack.shape[2])
    sg_w = wg[:, 0].reshape(n_seq * wpack.shape[1], wpack.shape[2])
    su_w = wg[:, 1].reshape(n_seq * wpack.shape[1], wpack.shape[2])
    sd_t = wg[:, 2].reshape(n_tp, n_seq // n_tp, wpack.shape[1], wpack.shape[2])
    sd_own = lax.all_to_all(sd_t, TP, split_axis=0, concat_axis=0, tiled=True)

    kv = jnp.concatenate([key_cache, key_new, value_cache, value_new], 0)
    kvg = gather_seq(kv).reshape(n_seq, kv.shape[0], HD)
    pos = jnp.arange(n_seq, dtype=jnp.int32)
    src = (pos % n_yh) * (n_z * n_c) + ((pos // n_yh) % n_z) * n_c + pos // (n_yh * n_z)
    ck = kvg[:, :block_rows].reshape(n_seq * block_rows, HD)
    nk = kvg[:, block_rows:block_rows + tok_rows].reshape(n_seq * tok_rows, HD)
    cv = kvg[:, block_rows + tok_rows:2 * block_rows + tok_rows].reshape(n_seq * block_rows, HD)
    nv = kvg[:, 2 * block_rows + tok_rows:].reshape(n_seq * tok_rows, HD)

    scale = 1.0 / math.sqrt(HD)
    s_c = jnp.dot(query, ck.T, preferred_element_type=jnp.float32) * scale
    s_n = jnp.dot(query, nk.T, preferred_element_type=jnp.float32) * scale
    c_open = (
        jnp.arange(block_rows, dtype=jnp.int32)[None, :] < cache_len[src][:, None]
    ).reshape(n_seq * block_rows)
    key_place = (src[:, None] * tok_rows + jnp.arange(tok_rows, dtype=jnp.int32)[None, :]).reshape(
        n_seq * tok_rows
    )
    query_place = seq_index * tok_rows + jnp.arange(tok_rows, dtype=jnp.int32)
    n_open = key_place[None, :] <= query_place[:, None]
    s_c = jnp.where(c_open[None, :], s_c, -jnp.inf)
    s_n = jnp.where(n_open, s_n, -jnp.inf)
    top = jnp.maximum(jnp.max(s_c, axis=-1, keepdims=True), jnp.max(s_n, axis=-1, keepdims=True))
    e_c = jnp.exp(s_c - top)
    e_n = jnp.exp(s_n - top)
    total = jnp.sum(e_c, axis=-1, keepdims=True) + jnp.sum(e_n, axis=-1, keepdims=True)
    p_c = (e_c / total).astype(jnp.bfloat16)
    p_n = (e_n / total).astype(jnp.bfloat16)
    attn = jnp.dot(p_c, cv, preferred_element_type=jnp.float32) + jnp.dot(
        p_n, nv, preferred_element_type=jnp.float32
    )
    attn = attn.astype(jnp.bfloat16)

    attn_blocks = tp_blocks(attn, n_tp)
    projected = sum(
        jnp.dot(a, w, preferred_element_type=jnp.float32) for a, w in zip(attn_blocks, ow_blocks)
    )
    hidden_state = resid.astype(jnp.float32) + projected
    mean_square = jnp.mean(hidden_state * hidden_state, axis=-1, keepdims=True)
    normed = (hidden_state * lax.rsqrt(mean_square + 1e-06) * norm_gain.astype(jnp.float32)).astype(
        jnp.bfloat16
    )
    own_hidden = lax.dynamic_slice_in_dim(hidden_state, tp_index * width, width, 1)
    own_normed = lax.dynamic_slice_in_dim(normed, tp_index * width, width, 1)

    logits = jnp.dot(normed, router, preferred_element_type=jnp.float32)
    expert_count = router.shape[1]
    expert_range = jnp.arange(expert_count, dtype=jnp.int32)
    picked = jnp.sum(
        jnp.where(expert_ids[:, :, None] == expert_range[None, None, :], logits[:, None, :], 0.0),
        axis=-1,
    )
    gates = jax.nn.softmax(picked, axis=-1)

    shared_gate = jnp.dot(normed, sg_w, preferred_element_type=jnp.float32)
    shared_up = jnp.dot(normed, su_w, preferred_element_type=jnp.float32)
    shared_inner = (jax.nn.silu(shared_gate) * shared_up).astype(jnp.bfloat16)
    shared_own = sum(
        jnp.einsum(
            "qf,sjf->qsj",
            b,
            lax.dynamic_index_in_dim(sd_own, (tp_index - k) % n_tp, 0, keepdims=False),
            preferred_element_type=jnp.float32,
        )
        for k, b in enumerate(tp_blocks(shared_inner, n_tp))
    ).reshape(tok_rows, width)

    flat_ids = expert_ids.reshape(tok_rows * TOPK)
    one_hot = (flat_ids[:, None] == expert_range[None, :]).astype(jnp.int32)
    before = jnp.cumsum(one_hot, axis=0) - one_hot
    slot = jnp.sum(one_hot * before, axis=1)
    dest = flat_ids * CAP + slot
    slots = expert_count * CAP
    place = (dest[None, :] == jnp.arange(slots, dtype=jnp.int32)[:, None]).reshape(
        slots, tok_rows, TOPK
    )
    dispatch = jnp.any(place, axis=-1).astype(jnp.bfloat16)
    buffer = jnp.dot(dispatch, own_normed, preferred_element_type=jnp.float32).astype(jnp.bfloat16)
    buffer = buffer.reshape(expert_count, CAP, width)
    recv = lax.all_to_all(buffer, SEQ, split_axis=0, concat_axis=0, tiled=True)
    ff = w_gate.shape[2]
    rows_flat = recv.reshape(slots, width)
    wg_b = w_gate[0].reshape(n_tp, width, ff)
    wu_b = w_up[0].reshape(n_tp, width, ff)
    wd_b = w_down[0].reshape(n_tp, ff, w_down.shape[2])
    gate_pre = 0.0
    up_pre = 0.0
    for k, b in enumerate(tp_blocks(rows_flat, n_tp)):
        src_tp = (tp_index - k) % n_tp
        gate_pre = gate_pre + jnp.dot(
            b, lax.dynamic_index_in_dim(wg_b, src_tp, 0, keepdims=False), preferred_element_type=jnp.float32
        )
        up_pre = up_pre + jnp.dot(
            b, lax.dynamic_index_in_dim(wu_b, src_tp, 0, keepdims=False), preferred_element_type=jnp.float32
        )
    inner = (jax.nn.silu(gate_pre) * up_pre).astype(jnp.bfloat16)
    out = 0.0
    for k, b in enumerate(tp_blocks(inner, n_tp)):
        src_tp = (tp_index - k) % n_tp
        out = out + jnp.dot(
            b, lax.dynamic_index_in_dim(wd_b, src_tp, 0, keepdims=False), preferred_element_type=jnp.float32
        )
    out = out.astype(jnp.bfloat16).reshape(expert_count, CAP, w_down.shape[2])
    returned = lax.all_to_all(out, SEQ, split_axis=0, concat_axis=0, tiled=True)
    picked_rows = returned.reshape(slots, width)[dest]
    weighted = picked_rows.astype(jnp.float32) * gates.reshape(tok_rows * TOPK)[:, None]
    routed = jnp.sum(weighted.reshape(tok_rows, TOPK, width), axis=1)
    return (own_hidden + shared_own + routed).astype(jnp.bfloat16)


def solution(mesh):
    n_seq, n_tp = mesh.devices.shape
    fine = Mesh(mesh.devices.reshape(n_seq // 16, 8, 2, n_tp // 2, 2), SEQ + TP)
    return jax.shard_map(
        local,
        mesh=fine,
        in_specs=(
            P(SEQ, None),
            P(SEQ, TP),
            P(SEQ, TP),
            P(SEQ, TP),
            P(SEQ, TP),
            P(SEQ, TP),
            P(),
            P(TP, None),
            P(),
            P(),
            P(SEQ, None),
            P(SEQ, None, TP),
            P(SEQ, None, TP),
            P(SEQ, None, TP),
            P(SEQ, TP),
            P(SEQ, TP),
            P(TP, SEQ),
        ),
        out_specs=P(SEQ, TP),
        check_vma=False,
    )
```

```python
import math

import jax
import jax.numpy as jnp
import numpy as np
from jax import lax
from jax.sharding import Mesh
from jax.sharding import PartitionSpec as P

D = 2048
HD = 128
TOPK = 6
CAP = 18

SEQ = ("yh", "z", "c")
TP = ("x", "yl")


def gather_seq(x):
    g = lax.all_gather(x, "yh", axis=0)
    g = lax.all_gather(g, "z", axis=0)
    g = lax.all_gather(g, "c", axis=0)
    return g


def tp_blocks(x, n_tp):
    out = [x]
    for k in range(1, n_tp):
        out.append(lax.ppermute(x, TP, [(j, (j + k) % n_tp) for j in range(n_tp)]))
    return out


def local(
    resid,
    query,
    key_new,
    value_new,
    key_cache,
    value_cache,
    cache_len,
    out_weight,
    norm_gain,
    router,
    expert_ids,
    w_gate,
    w_up,
    w_down,
    w_shared_gate,
    w_shared_up,
    w_shared_down,
):
    tok_rows = query.shape[0]
    block_rows = key_cache.shape[0]
    n_yh, n_z, n_c = (lax.axis_size(a) for a in SEQ)
    n_x, n_yl = (lax.axis_size(a) for a in TP)
    n_seq = n_yh * n_z * n_c
    n_tp = n_x * n_yl
    seq_index = (lax.axis_index("yh") * n_z + lax.axis_index("z")) * n_c + lax.axis_index("c")
    tp_index = lax.axis_index("x") * n_yl + lax.axis_index("yl")
    width = D // n_tp

    wpack = jnp.stack([w_shared_gate, w_shared_up, w_shared_down.T], 0)
    w_rows = wpack.size // HD
    kv = jnp.concatenate(
        [key_cache, key_new, value_cache, value_new, wpack.reshape(w_rows, HD)], 0
    )
    g = lax.all_gather(kv, "yh", axis=0)
    g = lax.all_gather(g, "z", axis=0)
    other = lax.ppermute(g, "c", [(0, 1), (1, 0)])
    kvg = jnp.stack([g, other], 0).reshape(n_seq, kv.shape[0], HD)
    my_c = lax.axis_index("c")
    pos = jnp.arange(n_seq, dtype=jnp.int32)
    src = (pos % n_yh) * (n_z * n_c) + ((pos // n_yh) % n_z) * n_c + (pos // (n_yh * n_z) + my_c) % n_c
    s_ids = jnp.arange(n_seq, dtype=jnp.int32)
    pos_of_s = ((s_ids % n_c - my_c) % n_c) * (n_yh * n_z) + ((s_ids // n_c) % n_z) * n_yh + s_ids // (n_c * n_z)
    kv_rows = 2 * (block_rows + tok_rows)
    wg = jnp.take(kvg[:, kv_rows:], pos_of_s, axis=0).reshape(n_seq, 3, wpack.shape[1], wpack.shape[2])
    sg_w = wg[:, 0].reshape(n_seq * wpack.shape[1], wpack.shape[2])
    su_w = wg[:, 1].reshape(n_seq * wpack.shape[1], wpack.shape[2])
    sd_t = wg[:, 2].reshape(n_tp, n_seq // n_tp, wpack.shape[1], wpack.shape[2])
    sd_own = lax.all_to_all(sd_t, TP, split_axis=0, concat_axis=0, tiled=True)
    ck = kvg[:, :block_rows].reshape(n_seq * block_rows, HD)
    nk = kvg[:, block_rows:block_rows + tok_rows].reshape(n_seq * tok_rows, HD)
    cv = kvg[:, block_rows + tok_rows:2 * block_rows + tok_rows].reshape(n_seq * block_rows, HD)
    nv = kvg[:, 2 * block_rows + tok_rows:kv_rows].reshape(n_seq * tok_rows, HD)

    scale = 1.0 / math.sqrt(HD)
    s_c = jnp.dot(query, ck.T, preferred_element_type=jnp.float32) * scale
    s_n = jnp.dot(query, nk.T, preferred_element_type=jnp.float32) * scale
    c_open = (
        jnp.arange(block_rows, dtype=jnp.int32)[None, :] < cache_len[src][:, None]
    ).reshape(n_seq * block_rows)
    key_place = (src[:, None] * tok_rows + jnp.arange(tok_rows, dtype=jnp.int32)[None, :]).reshape(
        n_seq * tok_rows
    )
    query_place = seq_index * tok_rows + jnp.arange(tok_rows, dtype=jnp.int32)
    n_open = key_place[None, :] <= query_place[:, None]
    s_c = jnp.where(c_open[None, :], s_c, -jnp.inf)
    s_n = jnp.where(n_open, s_n, -jnp.inf)
    top = jnp.maximum(jnp.max(s_c, axis=-1, keepdims=True), jnp.max(s_n, axis=-1, keepdims=True))
    e_c = jnp.exp(s_c - top)
    e_n = jnp.exp(s_n - top)
    total = jnp.sum(e_c, axis=-1, keepdims=True) + jnp.sum(e_n, axis=-1, keepdims=True)
    p_c = (e_c / total).astype(jnp.bfloat16)
    p_n = (e_n / total).astype(jnp.bfloat16)
    attn = jnp.dot(p_c, cv, preferred_element_type=jnp.float32) + jnp.dot(
        p_n, nv, preferred_element_type=jnp.float32
    )
    attn = attn.astype(jnp.bfloat16)

    paired = tp_blocks(jnp.concatenate([attn, out_weight], 1), n_tp)
    projected = sum(
        jnp.dot(b[:, :HD], b[:, HD:], preferred_element_type=jnp.float32) for b in paired
    )
    hidden_state = resid.astype(jnp.float32) + projected
    mean_square = jnp.mean(hidden_state * hidden_state, axis=-1, keepdims=True)
    normed = (hidden_state * lax.rsqrt(mean_square + 1e-06) * norm_gain.astype(jnp.float32)).astype(
        jnp.bfloat16
    )
    own_hidden = lax.dynamic_slice_in_dim(hidden_state, tp_index * width, width, 1)
    own_normed = lax.dynamic_slice_in_dim(normed, tp_index * width, width, 1)

    logits = jnp.dot(normed, router, preferred_element_type=jnp.float32)
    expert_count = router.shape[1]
    expert_range = jnp.arange(expert_count, dtype=jnp.int32)
    picked = jnp.sum(
        jnp.where(expert_ids[:, :, None] == expert_range[None, None, :], logits[:, None, :], 0.0),
        axis=-1,
    )
    gates = jax.nn.softmax(picked, axis=-1)

    shared_gate = jnp.dot(normed, sg_w, preferred_element_type=jnp.float32)
    shared_up = jnp.dot(normed, su_w, preferred_element_type=jnp.float32)
    shared_inner = (jax.nn.silu(shared_gate) * shared_up).astype(jnp.bfloat16)

    flat_ids = expert_ids.reshape(tok_rows * TOPK)
    one_hot = (flat_ids[:, None] == expert_range[None, :]).astype(jnp.int32)
    before = jnp.cumsum(one_hot, axis=0) - one_hot
    slot = jnp.sum(one_hot * before, axis=1)
    dest = flat_ids * CAP + slot
    slots = expert_count * CAP
    place = (dest[None, :] == jnp.arange(slots, dtype=jnp.int32)[:, None]).reshape(
        slots, tok_rows, TOPK
    )
    dispatch = jnp.any(place, axis=-1).astype(jnp.bfloat16)
    buffer = jnp.dot(dispatch, own_normed, preferred_element_type=jnp.float32).astype(jnp.bfloat16)
    buffer = buffer.reshape(expert_count, CAP, width)
    recv = lax.all_to_all(buffer, SEQ, split_axis=0, concat_axis=0, tiled=True)
    ff = w_gate.shape[2]
    rows_flat = recv.reshape(slots, width)
    inner_rows = shared_inner.size // width
    carried = jnp.concatenate([rows_flat, shared_inner.reshape(inner_rows, width)], 0)
    wg_b = w_gate[0].reshape(n_tp, width, ff)
    wu_b = w_up[0].reshape(n_tp, width, ff)
    wd_b = w_down[0].reshape(n_tp, ff, w_down.shape[2])
    gate_pre = 0.0
    up_pre = 0.0
    shared_own = 0.0
    for k, both in enumerate(tp_blocks(carried, n_tp)):
        src_tp = (tp_index - k) % n_tp
        b = both[:slots]
        shared_own = shared_own + jnp.einsum(
            "qf,sjf->qsj",
            both[slots:].reshape(shared_inner.shape),
            lax.dynamic_index_in_dim(sd_own, src_tp, 0, keepdims=False),
            preferred_element_type=jnp.float32,
        )
        gate_pre = gate_pre + jnp.dot(
            b, lax.dynamic_index_in_dim(wg_b, src_tp, 0, keepdims=False), preferred_element_type=jnp.float32
        )
        up_pre = up_pre + jnp.dot(
            b, lax.dynamic_index_in_dim(wu_b, src_tp, 0, keepdims=False), preferred_element_type=jnp.float32
        )
    inner = (jax.nn.silu(gate_pre) * up_pre).astype(jnp.bfloat16)
    out = 0.0
    for k, b in enumerate(tp_blocks(inner, n_tp)):
        src_tp = (tp_index - k) % n_tp
        out = out + jnp.dot(
            b, lax.dynamic_index_in_dim(wd_b, src_tp, 0, keepdims=False), preferred_element_type=jnp.float32
        )
    out = out.astype(jnp.bfloat16).reshape(expert_count, CAP, w_down.shape[2])
    shared_own = shared_own.reshape(tok_rows, width)
    returned = lax.all_to_all(out, SEQ, split_axis=0, concat_axis=0, tiled=True)
    picked_rows = returned.reshape(slots, width)[dest]
    weighted = picked_rows.astype(jnp.float32) * gates.reshape(tok_rows * TOPK)[:, None]
    routed = jnp.sum(weighted.reshape(tok_rows, TOPK, width), axis=1)
    return (own_hidden + shared_own + routed).astype(jnp.bfloat16)


def solution(mesh):
    n_seq, n_tp = mesh.devices.shape
    fine = Mesh(mesh.devices.reshape(n_seq // 16, 8, 2, n_tp // 2, 2), SEQ + TP)
    return jax.shard_map(
        local,
        mesh=fine,
        in_specs=(
            P(SEQ, None),
            P(SEQ, TP),
            P(SEQ, TP),
            P(SEQ, TP),
            P(SEQ, TP),
            P(SEQ, TP),
            P(),
            P(TP, None),
            P(),
            P(),
            P(SEQ, None),
            P(SEQ, None, TP),
            P(SEQ, None, TP),
            P(SEQ, None, TP),
            P(SEQ, TP),
            P(SEQ, TP),
            P(TP, SEQ),
        ),
        out_specs=P(SEQ, TP),
        check_vma=False,
    )
```

```python
import math

import jax
import jax.numpy as jnp
import numpy as np
from jax import lax
from jax.sharding import Mesh
from jax.sharding import PartitionSpec as P

D = 2048
HD = 128
TOPK = 6
CAP = 18

SEQ = ("yh", "z", "c")
TP = ("x", "yl")


def gather_seq(x):
    g = lax.all_gather(x, "yh", axis=0)
    g = lax.all_gather(g, "z", axis=0)
    g = lax.all_gather(g, "c", axis=0)
    return g


def tp_blocks(x, n_tp):
    out = [x]
    for k in range(1, n_tp):
        out.append(lax.ppermute(x, TP, [(j, (j + k) % n_tp) for j in range(n_tp)]))
    return out


def tp_gather(x, n_tp):
    b = jnp.broadcast_to(x[None], (n_tp,) + x.shape)
    return lax.all_to_all(b, TP, split_axis=0, concat_axis=0, tiled=True)


def local(
    resid,
    query,
    key_new,
    value_new,
    key_cache,
    value_cache,
    cache_len,
    out_weight,
    norm_gain,
    router,
    expert_ids,
    w_gate,
    w_up,
    w_down,
    w_shared_gate,
    w_shared_up,
    w_shared_down,
):
    tok_rows = query.shape[0]
    block_rows = key_cache.shape[0]
    n_yh, n_z, n_c = (lax.axis_size(a) for a in SEQ)
    n_x, n_yl = (lax.axis_size(a) for a in TP)
    n_seq = n_yh * n_z * n_c
    n_tp = n_x * n_yl
    seq_index = (lax.axis_index("yh") * n_z + lax.axis_index("z")) * n_c + lax.axis_index("c")
    tp_index = lax.axis_index("x") * n_yl + lax.axis_index("yl")
    width = D // n_tp

    wpack = jnp.stack([w_shared_gate, w_shared_up, w_shared_down.T], 0)
    w_rows = wpack.size // HD
    kv = jnp.concatenate(
        [key_cache, key_new, value_cache, value_new, wpack.reshape(w_rows, HD)], 0
    )
    g = lax.all_gather(kv, "yh", axis=0)
    g = lax.all_gather(g, "z", axis=0)
    other = lax.ppermute(g, "c", [(0, 1), (1, 0)])
    kvg = jnp.stack([g, other], 0).reshape(n_seq, kv.shape[0], HD)
    my_c = lax.axis_index("c")
    pos = jnp.arange(n_seq, dtype=jnp.int32)
    src = (pos % n_yh) * (n_z * n_c) + ((pos // n_yh) % n_z) * n_c + (pos // (n_yh * n_z) + my_c) % n_c
    s_ids = jnp.arange(n_seq, dtype=jnp.int32)
    pos_of_s = ((s_ids % n_c - my_c) % n_c) * (n_yh * n_z) + ((s_ids // n_c) % n_z) * n_yh + s_ids // (n_c * n_z)
    kv_rows = 2 * (block_rows + tok_rows)
    wg = jnp.take(kvg[:, kv_rows:], pos_of_s, axis=0).reshape(n_seq, 3, wpack.shape[1], wpack.shape[2])
    sg_w = wg[:, 0].reshape(n_seq * wpack.shape[1], wpack.shape[2])
    su_w = wg[:, 1].reshape(n_seq * wpack.shape[1], wpack.shape[2])
    sd_t = wg[:, 2].reshape(n_tp, n_seq // n_tp, wpack.shape[1], wpack.shape[2])
    ow_all = tp_gather(out_weight, n_tp)
    ck = kvg[:, :block_rows].reshape(n_seq * block_rows, HD)
    nk = kvg[:, block_rows:block_rows + tok_rows].reshape(n_seq * tok_rows, HD)
    cv = kvg[:, block_rows + tok_rows:2 * block_rows + tok_rows].reshape(n_seq * block_rows, HD)
    nv = kvg[:, 2 * block_rows + tok_rows:kv_rows].reshape(n_seq * tok_rows, HD)

    scale = 1.0 / math.sqrt(HD)
    s_c = jnp.dot(query, ck.T, preferred_element_type=jnp.float32) * scale
    s_n = jnp.dot(query, nk.T, preferred_element_type=jnp.float32) * scale
    c_open = (
        jnp.arange(block_rows, dtype=jnp.int32)[None, :] < cache_len[src][:, None]
    ).reshape(n_seq * block_rows)
    key_place = (src[:, None] * tok_rows + jnp.arange(tok_rows, dtype=jnp.int32)[None, :]).reshape(
        n_seq * tok_rows
    )
    query_place = seq_index * tok_rows + jnp.arange(tok_rows, dtype=jnp.int32)
    n_open = key_place[None, :] <= query_place[:, None]
    s_c = jnp.where(c_open[None, :], s_c, -jnp.inf)
    s_n = jnp.where(n_open, s_n, -jnp.inf)
    top = jnp.maximum(jnp.max(s_c, axis=-1, keepdims=True), jnp.max(s_n, axis=-1, keepdims=True))
    e_c = jnp.exp(s_c - top)
    e_n = jnp.exp(s_n - top)
    total = jnp.sum(e_c, axis=-1, keepdims=True) + jnp.sum(e_n, axis=-1, keepdims=True)
    p_c = (e_c / total).astype(jnp.bfloat16)
    p_n = (e_n / total).astype(jnp.bfloat16)
    attn = jnp.dot(p_c, cv, preferred_element_type=jnp.float32) + jnp.dot(
        p_n, nv, preferred_element_type=jnp.float32
    )
    attn = attn.astype(jnp.bfloat16)

    sd_rows = sd_t[0].size // HD
    mixed_in = jnp.concatenate(
        [jnp.broadcast_to(attn[None], (n_tp,) + attn.shape), sd_t.reshape(n_tp, sd_rows, HD)], 1
    )
    mixed_out = lax.all_to_all(mixed_in, TP, split_axis=0, concat_axis=0, tiled=True)
    attn_all = mixed_out[:, :tok_rows]
    sd_own = mixed_out[:, tok_rows:].reshape(sd_t.shape)
    projected = jnp.einsum("tqd,tdn->qn", attn_all, ow_all, preferred_element_type=jnp.float32)
    hidden_state = resid.astype(jnp.float32) + projected
    mean_square = jnp.mean(hidden_state * hidden_state, axis=-1, keepdims=True)
    normed = (hidden_state * lax.rsqrt(mean_square + 1e-06) * norm_gain.astype(jnp.float32)).astype(
        jnp.bfloat16
    )
    own_hidden = lax.dynamic_slice_in_dim(hidden_state, tp_index * width, width, 1)
    own_normed = lax.dynamic_slice_in_dim(normed, tp_index * width, width, 1)

    logits = jnp.dot(normed, router, preferred_element_type=jnp.float32)
    expert_count = router.shape[1]
    expert_range = jnp.arange(expert_count, dtype=jnp.int32)
    picked = jnp.sum(
        jnp.where(expert_ids[:, :, None] == expert_range[None, None, :], logits[:, None, :], 0.0),
        axis=-1,
    )
    gates = jax.nn.softmax(picked, axis=-1)

    shared_gate = jnp.dot(normed, sg_w, preferred_element_type=jnp.float32)
    shared_up = jnp.dot(normed, su_w, preferred_element_type=jnp.float32)
    shared_inner = (jax.nn.silu(shared_gate) * shared_up).astype(jnp.bfloat16)

    flat_ids = expert_ids.reshape(tok_rows * TOPK)
    one_hot = (flat_ids[:, None] == expert_range[None, :]).astype(jnp.int32)
    before = jnp.cumsum(one_hot, axis=0) - one_hot
    slot = jnp.sum(one_hot * before, axis=1)
    dest = flat_ids * CAP + slot
    slots = expert_count * CAP
    place = (dest[None, :] == jnp.arange(slots, dtype=jnp.int32)[:, None]).reshape(
        slots, tok_rows, TOPK
    )
    dispatch = jnp.any(place, axis=-1).astype(jnp.bfloat16)
    buffer = jnp.dot(dispatch, own_normed, preferred_element_type=jnp.float32).astype(jnp.bfloat16)
    buffer = buffer.reshape(expert_count, CAP, width)
    recv = lax.all_to_all(buffer, SEQ, split_axis=0, concat_axis=0, tiled=True)
    ff = w_gate.shape[2]
    rows_flat = recv.reshape(slots, width)
    inner_rows = shared_inner.size // width
    carried = jnp.concatenate([rows_flat, shared_inner.reshape(inner_rows, width)], 0)
    wg_b = w_gate[0].reshape(n_tp, width, ff)
    wu_b = w_up[0].reshape(n_tp, width, ff)
    wd_b = w_down[0].reshape(n_tp, ff, w_down.shape[2])
    both = tp_gather(carried, n_tp)
    rows_all = both[:, :slots]
    sinner_all = both[:, slots:].reshape((n_tp,) + shared_inner.shape)
    shared_own = jnp.einsum("tqf,tsjf->qsj", sinner_all, sd_own, preferred_element_type=jnp.float32)
    gate_pre = jnp.einsum("tsc,tcf->sf", rows_all, wg_b, preferred_element_type=jnp.float32)
    up_pre = jnp.einsum("tsc,tcf->sf", rows_all, wu_b, preferred_element_type=jnp.float32)
    inner = (jax.nn.silu(gate_pre) * up_pre).astype(jnp.bfloat16)
    inner_all = tp_gather(inner, n_tp)
    out = jnp.einsum("tsf,tfn->sn", inner_all, wd_b, preferred_element_type=jnp.float32)
    out = out.astype(jnp.bfloat16).reshape(expert_count, CAP, w_down.shape[2])
    shared_own = shared_own.reshape(tok_rows, width)
    returned = lax.all_to_all(out, SEQ, split_axis=0, concat_axis=0, tiled=True)
    picked_rows = returned.reshape(slots, width)[dest]
    weighted = picked_rows.astype(jnp.float32) * gates.reshape(tok_rows * TOPK)[:, None]
    routed = jnp.sum(weighted.reshape(tok_rows, TOPK, width), axis=1)
    return (own_hidden + shared_own + routed).astype(jnp.bfloat16)


def solution(mesh):
    n_seq, n_tp = mesh.devices.shape
    fine = Mesh(mesh.devices.reshape(n_seq // 16, 8, 2, n_tp // 2, 2), SEQ + TP)
    return jax.shard_map(
        local,
        mesh=fine,
        in_specs=(
            P(SEQ, None),
            P(SEQ, TP),
            P(SEQ, TP),
            P(SEQ, TP),
            P(SEQ, TP),
            P(SEQ, TP),
            P(),
            P(TP, None),
            P(),
            P(),
            P(SEQ, None),
            P(SEQ, None, TP),
            P(SEQ, None, TP),
            P(SEQ, None, TP),
            P(SEQ, TP),
            P(SEQ, TP),
            P(TP, SEQ),
        ),
        out_specs=P(SEQ, TP),
        check_vma=False,
    )
```

```python
import math

import jax
import jax.numpy as jnp
import numpy as np
from jax import lax
from jax.sharding import Mesh
from jax.sharding import PartitionSpec as P

D = 2048
HD = 128
TOPK = 6
CAP = 18

SEQ = ("yh", "z", "c")
TP = ("x", "yl")


def gather_seq(x):
    g = lax.all_gather(x, "yh", axis=0)
    g = lax.all_gather(g, "z", axis=0)
    g = lax.all_gather(g, "c", axis=0)
    return g


def tp_blocks(x, n_tp):
    out = [x]
    for k in range(1, n_tp):
        out.append(lax.ppermute(x, TP, [(j, (j + k) % n_tp) for j in range(n_tp)]))
    return out


def tp_gather(x, n_tp):
    b = jnp.broadcast_to(x[None], (n_tp,) + x.shape)
    return lax.all_to_all(b, TP, split_axis=0, concat_axis=0, tiled=True)


def local(
    resid,
    query,
    key_new,
    value_new,
    key_cache,
    value_cache,
    cache_len,
    out_weight,
    norm_gain,
    router,
    expert_ids,
    w_gate,
    w_up,
    w_down,
    w_shared_gate,
    w_shared_up,
    w_shared_down,
):
    tok_rows = query.shape[0]
    block_rows = key_cache.shape[0]
    n_yh, n_z, n_c = (lax.axis_size(a) for a in SEQ)
    n_x, n_yl = (lax.axis_size(a) for a in TP)
    n_seq = n_yh * n_z * n_c
    n_tp = n_x * n_yl
    seq_index = (lax.axis_index("yh") * n_z + lax.axis_index("z")) * n_c + lax.axis_index("c")
    tp_index = lax.axis_index("x") * n_yl + lax.axis_index("yl")
    width = D // n_tp

    kv = jnp.concatenate([key_cache, key_new, value_cache, value_new], 0)
    g = lax.all_gather(kv, ("yh", "z"), axis=0)
    other = lax.ppermute(g, "c", [(0, 1), (1, 0)])
    kvg = jnp.stack([g, other], 0).reshape(n_seq, kv.shape[0], HD)
    my_c = lax.axis_index("c")
    pos = jnp.arange(n_seq, dtype=jnp.int32)
    src = ((pos % (n_yh * n_z)) // n_z) * (n_z * n_c) + (pos % n_z) * n_c + (
        pos // (n_yh * n_z) + my_c
    ) % n_c
    s_ids = jnp.arange(n_seq, dtype=jnp.int32)
    pos_of_s = ((s_ids % n_c - my_c) % n_c) * (n_yh * n_z) + (s_ids // (n_c * n_z)) * n_z + (
        s_ids // n_c
    ) % n_z
    ck = kvg[:, :block_rows].reshape(n_seq * block_rows, HD)
    nk = kvg[:, block_rows:block_rows + tok_rows].reshape(n_seq * tok_rows, HD)
    cv = kvg[:, block_rows + tok_rows:2 * block_rows + tok_rows].reshape(n_seq * block_rows, HD)
    nv = kvg[:, 2 * block_rows + tok_rows:].reshape(n_seq * tok_rows, HD)

    wpack = jnp.stack([w_shared_gate, w_shared_up, w_shared_down.T], 0)
    w_rows = wpack.size // HD
    wflat = wpack.reshape(w_rows, HD) + (g[0, :1, :] * 0).astype(wpack.dtype)
    wgath = lax.all_gather(wflat, ("yh", "z"), axis=0)
    wother = lax.ppermute(wgath, "c", [(0, 1), (1, 0)])
    wk = jnp.stack([wgath, wother], 0).reshape(n_seq, w_rows, HD)
    wg = jnp.take(wk, pos_of_s, axis=0).reshape(n_seq, 3, wpack.shape[1], wpack.shape[2])
    sg_w = wg[:, 0].reshape(n_seq * wpack.shape[1], wpack.shape[2])
    su_w = wg[:, 1].reshape(n_seq * wpack.shape[1], wpack.shape[2])
    sd_t = wg[:, 2].reshape(n_tp, n_seq // n_tp, wpack.shape[1], wpack.shape[2])
    ow_all = tp_gather(out_weight, n_tp)

    scale = 1.0 / math.sqrt(HD)
    s_c = jnp.dot(query, ck.T, preferred_element_type=jnp.float32) * scale
    s_n = jnp.dot(query, nk.T, preferred_element_type=jnp.float32) * scale
    c_open = (
        jnp.arange(block_rows, dtype=jnp.int32)[None, :] < cache_len[src][:, None]
    ).reshape(n_seq * block_rows)
    key_place = (src[:, None] * tok_rows + jnp.arange(tok_rows, dtype=jnp.int32)[None, :]).reshape(
        n_seq * tok_rows
    )
    query_place = seq_index * tok_rows + jnp.arange(tok_rows, dtype=jnp.int32)
    n_open = key_place[None, :] <= query_place[:, None]
    s_c = jnp.where(c_open[None, :], s_c, -jnp.inf)
    s_n = jnp.where(n_open, s_n, -jnp.inf)
    top = jnp.maximum(jnp.max(s_c, axis=-1, keepdims=True), jnp.max(s_n, axis=-1, keepdims=True))
    e_c = jnp.exp(s_c - top)
    e_n = jnp.exp(s_n - top)
    total = jnp.sum(e_c, axis=-1, keepdims=True) + jnp.sum(e_n, axis=-1, keepdims=True)
    p_c = (e_c / total).astype(jnp.bfloat16)
    p_n = (e_n / total).astype(jnp.bfloat16)
    attn = jnp.dot(p_c, cv, preferred_element_type=jnp.float32) + jnp.dot(
        p_n, nv, preferred_element_type=jnp.float32
    )
    attn = attn.astype(jnp.bfloat16)

    sd_rows = sd_t[0].size // HD
    mixed_in = jnp.concatenate(
        [jnp.broadcast_to(attn[None], (n_tp,) + attn.shape), sd_t.reshape(n_tp, sd_rows, HD)], 1
    )
    mixed_out = lax.all_to_all(mixed_in, TP, split_axis=0, concat_axis=0, tiled=True)
    attn_all = mixed_out[:, :tok_rows]
    sd_own = mixed_out[:, tok_rows:].reshape(sd_t.shape)
    projected = jnp.einsum("tqd,tdn->qn", attn_all, ow_all, preferred_element_type=jnp.float32)
    hidden_state = resid.astype(jnp.float32) + projected
    mean_square = jnp.mean(hidden_state * hidden_state, axis=-1, keepdims=True)
    normed = (hidden_state * lax.rsqrt(mean_square + 1e-06) * norm_gain.astype(jnp.float32)).astype(
        jnp.bfloat16
    )
    own_hidden = lax.dynamic_slice_in_dim(hidden_state, tp_index * width, width, 1)
    own_normed = lax.dynamic_slice_in_dim(normed, tp_index * width, width, 1)

    logits = jnp.dot(normed, router, preferred_element_type=jnp.float32)
    expert_count = router.shape[1]
    expert_range = jnp.arange(expert_count, dtype=jnp.int32)
    picked = jnp.sum(
        jnp.where(expert_ids[:, :, None] == expert_range[None, None, :], logits[:, None, :], 0.0),
        axis=-1,
    )
    gates = jax.nn.softmax(picked, axis=-1)

    shared_gate = jnp.dot(normed, sg_w, preferred_element_type=jnp.float32)
    shared_up = jnp.dot(normed, su_w, preferred_element_type=jnp.float32)
    shared_inner = (jax.nn.silu(shared_gate) * shared_up).astype(jnp.bfloat16)

    flat_ids = expert_ids.reshape(tok_rows * TOPK)
    one_hot = (flat_ids[:, None] == expert_range[None, :]).astype(jnp.int32)
    before = jnp.cumsum(one_hot, axis=0) - one_hot
    slot = jnp.sum(one_hot * before, axis=1)
    dest = flat_ids * CAP + slot
    slots = expert_count * CAP
    place = (dest[None, :] == jnp.arange(slots, dtype=jnp.int32)[:, None]).reshape(
        slots, tok_rows, TOPK
    )
    dispatch = jnp.any(place, axis=-1).astype(jnp.bfloat16)
    buffer = jnp.dot(dispatch, own_normed, preferred_element_type=jnp.float32).astype(jnp.bfloat16)
    buffer = buffer.reshape(expert_count, CAP, width)
    recv = lax.all_to_all(buffer, SEQ, split_axis=0, concat_axis=0, tiled=True)
    ff = w_gate.shape[2]
    rows_flat = recv.reshape(slots, width)
    inner_rows = shared_inner.size // width
    carried = jnp.concatenate([rows_flat, shared_inner.reshape(inner_rows, width)], 0)
    wg_b = w_gate[0].reshape(n_tp, width, ff)
    wu_b = w_up[0].reshape(n_tp, width, ff)
    wd_b = w_down[0].reshape(n_tp, ff, w_down.shape[2])
    both = tp_gather(carried, n_tp)
    rows_all = both[:, :slots]
    sinner_all = both[:, slots:].reshape((n_tp,) + shared_inner.shape)
    shared_own = jnp.einsum("tqf,tsjf->qsj", sinner_all, sd_own, preferred_element_type=jnp.float32)
    gate_pre = jnp.einsum("tsc,tcf->sf", rows_all, wg_b, preferred_element_type=jnp.float32)
    up_pre = jnp.einsum("tsc,tcf->sf", rows_all, wu_b, preferred_element_type=jnp.float32)
    inner = (jax.nn.silu(gate_pre) * up_pre).astype(jnp.bfloat16)
    inner_all = tp_gather(inner, n_tp)
    out = jnp.einsum("tsf,tfn->sn", inner_all, wd_b, preferred_element_type=jnp.float32)
    out = out.astype(jnp.bfloat16).reshape(expert_count, CAP, w_down.shape[2])
    shared_own = shared_own.reshape(tok_rows, width)
    returned = lax.all_to_all(out, SEQ, split_axis=0, concat_axis=0, tiled=True)
    picked_rows = returned.reshape(slots, width)[dest]
    weighted = picked_rows.astype(jnp.float32) * gates.reshape(tok_rows * TOPK)[:, None]
    routed = jnp.sum(weighted.reshape(tok_rows, TOPK, width), axis=1)
    return (own_hidden + shared_own + routed).astype(jnp.bfloat16)


def solution(mesh):
    n_seq, n_tp = mesh.devices.shape
    fine = Mesh(mesh.devices.reshape(n_seq // 16, 8, 2, n_tp // 2, 2), SEQ + TP)
    return jax.shard_map(
        local,
        mesh=fine,
        in_specs=(
            P(SEQ, None),
            P(SEQ, TP),
            P(SEQ, TP),
            P(SEQ, TP),
            P(SEQ, TP),
            P(SEQ, TP),
            P(),
            P(TP, None),
            P(),
            P(),
            P(SEQ, None),
            P(SEQ, None, TP),
            P(SEQ, None, TP),
            P(SEQ, None, TP),
            P(SEQ, TP),
            P(SEQ, TP),
            P(TP, SEQ),
        ),
        out_specs=P(SEQ, TP),
        check_vma=False,
    )
```

```python
import functools
import math

import jax
import jax.numpy as jnp
import numpy as np
from jax import lax
from jax.sharding import Mesh
from jax.sharding import PartitionSpec as P

D = 2048
HD = 128
TOPK = 6
CAP = 18

SEQ = ("yh", "z", "c")
TP = ("x", "yl")


def gather_seq(x):
    g = lax.all_gather(x, "yh", axis=0)
    g = lax.all_gather(g, "z", axis=0)
    g = lax.all_gather(g, "c", axis=0)
    return g


def tp_blocks(x, n_tp):
    out = [x]
    for k in range(1, n_tp):
        out.append(lax.ppermute(x, TP, [(j, (j + k) % n_tp) for j in range(n_tp)]))
    return out


def tp_gather(x, n_tp):
    b = jnp.broadcast_to(x[None], (n_tp,) + x.shape)
    return lax.all_to_all(b, TP, split_axis=0, concat_axis=0, tiled=True)


def local(
    resid,
    query,
    key_new,
    value_new,
    key_cache,
    value_cache,
    cache_len,
    out_weight,
    norm_gain,
    router,
    expert_ids,
    w_gate,
    w_up,
    w_down,
    w_shared_gate,
    w_shared_up,
    w_shared_down,
):
    tok_rows = query.shape[0]
    block_rows = key_cache.shape[0]
    n_yh, n_z, n_c = (lax.axis_size(a) for a in SEQ)
    n_x, n_yl = (lax.axis_size(a) for a in TP)
    n_seq = n_yh * n_z * n_c
    n_tp = n_x * n_yl
    seq_index = (lax.axis_index("yh") * n_z + lax.axis_index("z")) * n_c + lax.axis_index("c")
    tp_index = lax.axis_index("x") * n_yl + lax.axis_index("yl")
    width = D // n_tp

    wpack = jnp.stack([w_shared_gate, w_shared_up, w_shared_down.T], 0)
    w_rows = wpack.size // HD
    kv = jnp.concatenate(
        [key_cache, key_new, value_cache, value_new, wpack.reshape(w_rows, HD)], 0
    )
    g = lax.all_gather(kv, "yh", axis=0)
    g = lax.all_gather(g, "z", axis=0).reshape(n_z * n_yh, kv.shape[0], HD)
    other = lax.ppermute(g, "c", [(0, 1), (1, 0)])
    my_c = lax.axis_index("c")
    kv_rows = 2 * (block_rows + tok_rows)
    first = my_c == 0
    w_c0 = jnp.where(first, g[:, kv_rows:], other[:, kv_rows:])
    w_c1 = jnp.where(first, other[:, kv_rows:], g[:, kv_rows:])
    wk = jnp.stack([w_c0, w_c1], 0).reshape(n_c, n_z, n_yh, w_rows, HD)
    wg = jnp.transpose(wk, (2, 1, 0, 3, 4)).reshape(n_seq, 3, wpack.shape[1], wpack.shape[2])
    sg_w = wg[:, 0].reshape(n_seq * wpack.shape[1], wpack.shape[2])
    su_w = wg[:, 1].reshape(n_seq * wpack.shape[1], wpack.shape[2])
    sd_t = wg[:, 2].reshape(n_tp, n_seq // n_tp, wpack.shape[1], wpack.shape[2])
    ow_all = tp_gather(out_weight, n_tp)

    scale = 1.0 / math.sqrt(HD)
    pos = jnp.arange(n_z * n_yh, dtype=jnp.int32)
    query_place = seq_index * tok_rows + jnp.arange(tok_rows, dtype=jnp.int32)
    halves = []
    for part, c_of in ((g, my_c), (other, 1 - my_c)):
        src = (pos % n_yh) * (n_z * n_c) + (pos // n_yh) * n_c + c_of
        ck = part[:, :block_rows].reshape(-1, HD)
        nk = part[:, block_rows:block_rows + tok_rows].reshape(-1, HD)
        cv = part[:, block_rows + tok_rows:2 * block_rows + tok_rows].reshape(-1, HD)
        nv = part[:, 2 * block_rows + tok_rows:kv_rows].reshape(-1, HD)
        s_c = jnp.dot(query, ck.T, preferred_element_type=jnp.float32) * scale
        s_n = jnp.dot(query, nk.T, preferred_element_type=jnp.float32) * scale
        c_open = (
            jnp.arange(block_rows, dtype=jnp.int32)[None, :] < cache_len[src][:, None]
        ).reshape(-1)
        key_place = (src[:, None] * tok_rows + jnp.arange(tok_rows, dtype=jnp.int32)[None, :]).reshape(-1)
        s_c = jnp.where(c_open[None, :], s_c, -jnp.inf)
        s_n = jnp.where(key_place[None, :] <= query_place[:, None], s_n, -jnp.inf)
        halves.append((s_c, s_n, cv, nv))
    top = functools.reduce(
        jnp.maximum, [jnp.max(x, axis=-1, keepdims=True) for h in halves for x in h[:2]]
    )
    exps = [(jnp.exp(h[0] - top), jnp.exp(h[1] - top)) for h in halves]
    total = sum(jnp.sum(x, axis=-1, keepdims=True) for e in exps for x in e)
    attn = sum(
        jnp.dot((e_c / total).astype(jnp.bfloat16), h[2], preferred_element_type=jnp.float32)
        + jnp.dot((e_n / total).astype(jnp.bfloat16), h[3], preferred_element_type=jnp.float32)
        for (e_c, e_n), h in zip(exps, halves)
    )
    attn = attn.astype(jnp.bfloat16)

    sd_rows = sd_t[0].size // HD
    mixed_in = jnp.concatenate(
        [jnp.broadcast_to(attn[None], (n_tp,) + attn.shape), sd_t.reshape(n_tp, sd_rows, HD)], 1
    )
    mixed_out = lax.all_to_all(mixed_in, TP, split_axis=0, concat_axis=0, tiled=True)
    attn_all = mixed_out[:, :tok_rows]
    sd_own = mixed_out[:, tok_rows:].reshape(sd_t.shape)
    projected = jnp.einsum("tqd,tdn->qn", attn_all, ow_all, preferred_element_type=jnp.float32)
    hidden_state = resid.astype(jnp.float32) + projected
    mean_square = jnp.mean(hidden_state * hidden_state, axis=-1, keepdims=True)
    normed = (hidden_state * lax.rsqrt(mean_square + 1e-06) * norm_gain.astype(jnp.float32)).astype(
        jnp.bfloat16
    )
    own_hidden = lax.dynamic_slice_in_dim(hidden_state, tp_index * width, width, 1)
    own_normed = lax.dynamic_slice_in_dim(normed, tp_index * width, width, 1)

    logits = jnp.dot(normed, router, preferred_element_type=jnp.float32)
    expert_count = router.shape[1]
    expert_range = jnp.arange(expert_count, dtype=jnp.int32)
    picked = jnp.sum(
        jnp.where(expert_ids[:, :, None] == expert_range[None, None, :], logits[:, None, :], 0.0),
        axis=-1,
    )
    gates = jax.nn.softmax(picked, axis=-1)

    shared_gate = jnp.dot(normed, sg_w, preferred_element_type=jnp.float32)
    shared_up = jnp.dot(normed, su_w, preferred_element_type=jnp.float32)
    shared_inner = (jax.nn.silu(shared_gate) * shared_up).astype(jnp.bfloat16)

    flat_ids = expert_ids.reshape(tok_rows * TOPK)
    one_hot = (flat_ids[:, None] == expert_range[None, :]).astype(jnp.int32)
    before = jnp.cumsum(one_hot, axis=0) - one_hot
    slot = jnp.sum(one_hot * before, axis=1)
    dest = flat_ids * CAP + slot
    slots = expert_count * CAP
    place = (dest[None, :] == jnp.arange(slots, dtype=jnp.int32)[:, None]).reshape(
        slots, tok_rows, TOPK
    )
    dispatch = jnp.any(place, axis=-1).astype(jnp.bfloat16)
    buffer = jnp.dot(dispatch, own_normed, preferred_element_type=jnp.float32).astype(jnp.bfloat16)
    buffer = buffer.reshape(expert_count, CAP, width)
    recv = lax.all_to_all(buffer, SEQ, split_axis=0, concat_axis=0, tiled=True)
    ff = w_gate.shape[2]
    rows_flat = recv.reshape(slots, width)
    inner_rows = shared_inner.size // width
    carried = jnp.concatenate([rows_flat, shared_inner.reshape(inner_rows, width)], 0)
    wg_b = w_gate[0].reshape(n_tp, width, ff)
    wu_b = w_up[0].reshape(n_tp, width, ff)
    wd_b = w_down[0].reshape(n_tp, ff, w_down.shape[2])
    both = tp_gather(carried, n_tp)
    rows_all = both[:, :slots]
    sinner_all = both[:, slots:].reshape((n_tp,) + shared_inner.shape)
    shared_own = jnp.einsum("tqf,tsjf->qsj", sinner_all, sd_own, preferred_element_type=jnp.float32)
    gate_pre = jnp.einsum("tsc,tcf->sf", rows_all, wg_b, preferred_element_type=jnp.float32)
    up_pre = jnp.einsum("tsc,tcf->sf", rows_all, wu_b, preferred_element_type=jnp.float32)
    inner = (jax.nn.silu(gate_pre) * up_pre).astype(jnp.bfloat16)
    inner_all = tp_gather(inner, n_tp)
    out = jnp.einsum("tsf,tfn->sn", inner_all, wd_b, preferred_element_type=jnp.float32)
    out = out.astype(jnp.bfloat16).reshape(expert_count, CAP, w_down.shape[2])
    shared_own = shared_own.reshape(tok_rows, width)
    returned = lax.all_to_all(out, SEQ, split_axis=0, concat_axis=0, tiled=True)
    picked_rows = returned.reshape(slots, width)[dest]
    weighted = picked_rows.astype(jnp.float32) * gates.reshape(tok_rows * TOPK)[:, None]
    routed = jnp.sum(weighted.reshape(tok_rows, TOPK, width), axis=1)
    return (own_hidden + shared_own + routed).astype(jnp.bfloat16)


def solution(mesh):
    n_seq, n_tp = mesh.devices.shape
    fine = Mesh(mesh.devices.reshape(n_seq // 16, 8, 2, n_tp // 2, 2), SEQ + TP)
    return jax.shard_map(
        local,
        mesh=fine,
        in_specs=(
            P(SEQ, None),
            P(SEQ, TP),
            P(SEQ, TP),
            P(SEQ, TP),
            P(SEQ, TP),
            P(SEQ, TP),
            P(),
            P(TP, None),
            P(),
            P(),
            P(SEQ, None),
            P(SEQ, None, TP),
            P(SEQ, None, TP),
            P(SEQ, None, TP),
            P(SEQ, TP),
            P(SEQ, TP),
            P(TP, SEQ),
        ),
        out_specs=P(SEQ, TP),
        check_vma=False,
    )
```

```python
import math

import jax
import jax.numpy as jnp
from jax import lax
from jax.sharding import Mesh
from jax.sharding import PartitionSpec as P


D = 2048
HD = 128
TOPK = 6
CAP = 18

SEQ = ("yh", "z", "c")
TP = ("x", "yl")


def tp_gather(x, n_tp):
    b = jnp.broadcast_to(x[None], (n_tp,) + x.shape)
    return lax.all_to_all(b, TP, split_axis=0, concat_axis=0, tiled=True)


def local(
    resid,
    query,
    key_new,
    value_new,
    key_cache,
    value_cache,
    cache_len,
    out_weight,
    norm_gain,
    router,
    expert_ids,
    w_gate,
    w_up,
    w_down,
    w_shared_gate,
    w_shared_up,
    w_shared_down,
):
    tok_rows = query.shape[0]
    block_rows = key_cache.shape[0]
    n_yh, n_z, n_c = (lax.axis_size(a) for a in SEQ)
    n_x, n_yl = (lax.axis_size(a) for a in TP)
    n_seq = n_yh * n_z * n_c
    n_tp = n_x * n_yl
    seq_index = (lax.axis_index("yh") * n_z + lax.axis_index("z")) * n_c + lax.axis_index("c")
    tp_index = lax.axis_index("x") * n_yl + lax.axis_index("yl")
    width = D // n_tp

    wpack = jnp.stack([w_shared_gate, w_shared_up, w_shared_down.T], 0)
    w_rows = wpack.size // HD
    kv = jnp.concatenate(
        [key_cache, key_new, value_cache, value_new, wpack.reshape(w_rows, HD)], 0
    )
    g = lax.all_gather(kv, "yh", axis=0)
    g = lax.all_gather(g, "z", axis=0)
    other = lax.ppermute(g, "c", [(0, 1), (1, 0)])
    kvg = jnp.stack([g, other], 0).reshape(n_seq, kv.shape[0], HD)
    my_c = lax.axis_index("c")
    pos = jnp.arange(n_seq, dtype=jnp.int32)
    src = (pos % n_yh) * (n_z * n_c) + ((pos // n_yh) % n_z) * n_c + (pos // (n_yh * n_z) + my_c) % n_c
    s_ids = jnp.arange(n_seq, dtype=jnp.int32)
    pos_of_s = ((s_ids % n_c - my_c) % n_c) * (n_yh * n_z) + ((s_ids // n_c) % n_z) * n_yh + s_ids // (n_c * n_z)
    kv_rows = 2 * (block_rows + tok_rows)
    wg = jnp.take(kvg[:, kv_rows:], pos_of_s, axis=0).reshape(n_seq, 3, wpack.shape[1], wpack.shape[2])
    sg_w = wg[:, 0].reshape(n_seq * wpack.shape[1], wpack.shape[2])
    su_w = wg[:, 1].reshape(n_seq * wpack.shape[1], wpack.shape[2])
    sd_t = wg[:, 2].reshape(n_tp, n_seq // n_tp, wpack.shape[1], wpack.shape[2])
    ow_all = tp_gather(out_weight, n_tp)
    ck = kvg[:, :block_rows].reshape(n_seq * block_rows, HD)
    nk = kvg[:, block_rows:block_rows + tok_rows].reshape(n_seq * tok_rows, HD)
    cv = kvg[:, block_rows + tok_rows:2 * block_rows + tok_rows].reshape(n_seq * block_rows, HD)
    nv = kvg[:, 2 * block_rows + tok_rows:kv_rows].reshape(n_seq * tok_rows, HD)

    scale = 1.0 / math.sqrt(HD)
    s_c = jnp.dot(query, ck.T, preferred_element_type=jnp.float32) * scale
    s_n = jnp.dot(query, nk.T, preferred_element_type=jnp.float32) * scale
    c_open = (
        jnp.arange(block_rows, dtype=jnp.int32)[None, :] < cache_len[src][:, None]
    ).reshape(n_seq * block_rows)
    key_place = (src[:, None] * tok_rows + jnp.arange(tok_rows, dtype=jnp.int32)[None, :]).reshape(
        n_seq * tok_rows
    )
    query_place = seq_index * tok_rows + jnp.arange(tok_rows, dtype=jnp.int32)
    n_open = key_place[None, :] <= query_place[:, None]
    s_c = jnp.where(c_open[None, :], s_c, -jnp.inf)
    s_n = jnp.where(n_open, s_n, -jnp.inf)
    top = jnp.maximum(jnp.max(s_c, axis=-1, keepdims=True), jnp.max(s_n, axis=-1, keepdims=True))
    e_c = jnp.exp(s_c - top)
    e_n = jnp.exp(s_n - top)
    total = jnp.sum(e_c, axis=-1, keepdims=True) + jnp.sum(e_n, axis=-1, keepdims=True)
    p_c = (e_c / total).astype(jnp.bfloat16)
    p_n = (e_n / total).astype(jnp.bfloat16)
    attn = jnp.dot(p_c, cv, preferred_element_type=jnp.float32) + jnp.dot(
        p_n, nv, preferred_element_type=jnp.float32
    )
    attn = attn.astype(jnp.bfloat16)

    sd_rows = sd_t[0].size // HD
    mixed_in = jnp.concatenate(
        [jnp.broadcast_to(attn[None], (n_tp,) + attn.shape), sd_t.reshape(n_tp, sd_rows, HD)], 1
    )
    mixed_out = lax.all_to_all(mixed_in, TP, split_axis=0, concat_axis=0, tiled=True)
    attn_all = mixed_out[:, :tok_rows]
    sd_own = mixed_out[:, tok_rows:].reshape(sd_t.shape)
    projected = jnp.einsum("tqd,tdn->qn", attn_all, ow_all, preferred_element_type=jnp.float32)
    hidden_state = resid.astype(jnp.float32) + projected
    mean_square = jnp.mean(hidden_state * hidden_state, axis=-1, keepdims=True)
    normed = (hidden_state * lax.rsqrt(mean_square + 1e-06) * norm_gain.astype(jnp.float32)).astype(
        jnp.bfloat16
    )
    own_hidden = lax.dynamic_slice_in_dim(hidden_state, tp_index * width, width, 1)
    own_normed = lax.dynamic_slice_in_dim(normed, tp_index * width, width, 1)

    logits = jnp.dot(normed, router, preferred_element_type=jnp.float32)
    expert_count = router.shape[1]
    expert_range = jnp.arange(expert_count, dtype=jnp.int32)
    picked = jnp.sum(
        jnp.where(expert_ids[:, :, None] == expert_range[None, None, :], logits[:, None, :], 0.0),
        axis=-1,
    )
    gates = jax.nn.softmax(picked, axis=-1)

    shared_gate = jnp.dot(normed, sg_w, preferred_element_type=jnp.float32)
    shared_up = jnp.dot(normed, su_w, preferred_element_type=jnp.float32)
    shared_inner = (jax.nn.silu(shared_gate) * shared_up).astype(jnp.bfloat16)

    flat_ids = expert_ids.reshape(tok_rows * TOPK)
    one_hot = (flat_ids[:, None] == expert_range[None, :]).astype(jnp.int32)
    before = jnp.cumsum(one_hot, axis=0) - one_hot
    slot = jnp.sum(one_hot * before, axis=1)
    dest = flat_ids * CAP + slot
    slots = expert_count * CAP
    place = (dest[None, :] == jnp.arange(slots, dtype=jnp.int32)[:, None]).reshape(
        slots, tok_rows, TOPK
    )
    dispatch = jnp.any(place, axis=-1).astype(jnp.bfloat16)
    buffer = jnp.dot(dispatch, own_normed, preferred_element_type=jnp.float32).astype(jnp.bfloat16)
    buffer = buffer.reshape(expert_count, CAP, width)
    recv = lax.all_to_all(buffer, SEQ, split_axis=0, concat_axis=0, tiled=True)
    ff = w_gate.shape[2]
    rows_flat = recv.reshape(slots, width)
    inner_rows = shared_inner.size // width
    carried = jnp.concatenate([rows_flat, shared_inner.reshape(inner_rows, width)], 0)
    wg_b = w_gate[0].reshape(n_tp, width, ff)
    wu_b = w_up[0].reshape(n_tp, width, ff)
    wd_b = w_down[0].reshape(n_tp, ff, w_down.shape[2])
    both = tp_gather(carried, n_tp)
    rows_all = both[:, :slots]
    sinner_all = both[:, slots:].reshape((n_tp,) + shared_inner.shape)
    shared_own = jnp.einsum("tqf,tsjf->qsj", sinner_all, sd_own, preferred_element_type=jnp.float32)
    gate_pre = jnp.einsum("tsc,tcf->sf", rows_all, wg_b, preferred_element_type=jnp.float32)
    up_pre = jnp.einsum("tsc,tcf->sf", rows_all, wu_b, preferred_element_type=jnp.float32)
    inner = (jax.nn.silu(gate_pre) * up_pre).astype(jnp.bfloat16)
    inner_all = tp_gather(inner, n_tp)
    out = jnp.einsum("tsf,tfn->sn", inner_all, wd_b, preferred_element_type=jnp.float32)
    out = out.astype(jnp.bfloat16).reshape(expert_count, CAP, w_down.shape[2])
    shared_own = shared_own.reshape(tok_rows, width)
    returned = lax.all_to_all(out, SEQ, split_axis=0, concat_axis=0, tiled=True)
    picked_rows = returned.reshape(slots, width)[dest]
    weighted = picked_rows.astype(jnp.float32) * gates.reshape(tok_rows * TOPK)[:, None]
    routed = jnp.sum(weighted.reshape(tok_rows, TOPK, width), axis=1)
    return (own_hidden + shared_own + routed).astype(jnp.bfloat16)


def solution(mesh):
    n_seq, n_tp = mesh.devices.shape
    fine = Mesh(mesh.devices.reshape(n_seq // 16, 8, 2, n_tp // 2, 2), SEQ + TP)
    return jax.shard_map(
        local,
        mesh=fine,
        in_specs=(
            P(SEQ, None),
            P(SEQ, TP),
            P(SEQ, TP),
            P(SEQ, TP),
            P(SEQ, TP),
            P(SEQ, TP),
            P(),
            P(TP, None),
            P(),
            P(),
            P(SEQ, None),
            P(SEQ, None, TP),
            P(SEQ, None, TP),
            P(SEQ, None, TP),
            P(SEQ, TP),
            P(SEQ, TP),
            P(TP, SEQ),
        ),
        out_specs=P(SEQ, TP),
        check_vma=False,
    )
```

```python
import functools
import math

import jax
import jax.numpy as jnp
from jax import lax
from jax.sharding import Mesh
from jax.sharding import PartitionSpec as P


D = 2048
HD = 128
TOPK = 6
CAP = 18

SEQ = ("yh", "z", "c")
TP = ("x", "yl")


def tp_gather(x, n_tp):
    b = jnp.broadcast_to(x[None], (n_tp,) + x.shape)
    return lax.all_to_all(b, TP, split_axis=0, concat_axis=0, tiled=True)


def local(
    resid,
    query,
    key_new,
    value_new,
    key_cache,
    value_cache,
    cache_len,
    out_weight,
    norm_gain,
    router,
    expert_ids,
    w_gate,
    w_up,
    w_down,
    w_shared_gate,
    w_shared_up,
    w_shared_down,
):
    tok_rows = query.shape[0]
    block_rows = key_cache.shape[0]
    n_yh, n_z, n_c = (lax.axis_size(a) for a in SEQ)
    n_x, n_yl = (lax.axis_size(a) for a in TP)
    n_seq = n_yh * n_z * n_c
    n_tp = n_x * n_yl
    seq_index = (lax.axis_index("yh") * n_z + lax.axis_index("z")) * n_c + lax.axis_index("c")
    tp_index = lax.axis_index("x") * n_yl + lax.axis_index("yl")
    width = D // n_tp

    wpack = jnp.stack([w_shared_gate, w_shared_up, w_shared_down.T], 0)
    w_rows = wpack.size // HD
    kv = jnp.concatenate(
        [key_cache, key_new, value_cache, value_new, wpack.reshape(w_rows, HD)], 0
    )
    g = lax.all_gather(kv, "yh", axis=0)
    g = lax.all_gather(g, "z", axis=0)
    g = g.reshape(n_z * n_yh, kv.shape[0], HD)
    other = lax.ppermute(g, "c", [(0, 1), (1, 0)])
    my_c = lax.axis_index("c")
    kv_rows = 2 * (block_rows + tok_rows)
    first = my_c == 0
    w_c0 = jnp.where(first, g[:, kv_rows:], other[:, kv_rows:])
    w_c1 = jnp.where(first, other[:, kv_rows:], g[:, kv_rows:])
    wk = jnp.stack([w_c0, w_c1], 0).reshape(n_c, n_z, n_yh, w_rows, HD)
    wg = jnp.transpose(wk, (2, 1, 0, 3, 4)).reshape(n_seq, 3, wpack.shape[1], wpack.shape[2])
    sg_w = wg[:, 0].reshape(n_seq * wpack.shape[1], wpack.shape[2])
    su_w = wg[:, 1].reshape(n_seq * wpack.shape[1], wpack.shape[2])
    sd_t = wg[:, 2].reshape(n_tp, n_seq // n_tp, wpack.shape[1], wpack.shape[2])
    ow_all = tp_gather(out_weight, n_tp)

    scale = 1.0 / math.sqrt(HD)
    pos = jnp.arange(n_z * n_yh, dtype=jnp.int32)
    query_place = seq_index * tok_rows + jnp.arange(tok_rows, dtype=jnp.int32)
    halves = []
    for part, c_of in ((g, my_c), (other, 1 - my_c)):
        src = (pos % n_yh) * (n_z * n_c) + (pos // n_yh) * n_c + c_of
        ck = part[:, :block_rows].reshape(-1, HD)
        nk = part[:, block_rows:block_rows + tok_rows].reshape(-1, HD)
        cv = part[:, block_rows + tok_rows:2 * block_rows + tok_rows].reshape(-1, HD)
        nv = part[:, 2 * block_rows + tok_rows:kv_rows].reshape(-1, HD)
        s_c = jnp.dot(query, ck.T, preferred_element_type=jnp.float32) * scale
        s_n = jnp.dot(query, nk.T, preferred_element_type=jnp.float32) * scale
        c_open = (
            jnp.arange(block_rows, dtype=jnp.int32)[None, :] < cache_len[src][:, None]
        ).reshape(-1)
        key_place = (src[:, None] * tok_rows + jnp.arange(tok_rows, dtype=jnp.int32)[None, :]).reshape(-1)
        s_c = jnp.where(c_open[None, :], s_c, -jnp.inf)
        s_n = jnp.where(key_place[None, :] <= query_place[:, None], s_n, -jnp.inf)
        halves.append((s_c, s_n, cv, nv))
    top = functools.reduce(
        jnp.maximum, [jnp.max(x, axis=-1, keepdims=True) for h in halves for x in h[:2]]
    )
    exps = [(jnp.exp(h[0] - top), jnp.exp(h[1] - top)) for h in halves]
    total = sum(jnp.sum(x, axis=-1, keepdims=True) for e in exps for x in e)
    attn = sum(
        jnp.dot((e_c / total).astype(jnp.bfloat16), h[2], preferred_element_type=jnp.float32)
        + jnp.dot((e_n / total).astype(jnp.bfloat16), h[3], preferred_element_type=jnp.float32)
        for (e_c, e_n), h in zip(exps, halves)
    )
    attn = attn.astype(jnp.bfloat16)

    sd_rows = sd_t[0].size // HD
    mixed_in = jnp.concatenate(
        [jnp.broadcast_to(attn[None], (n_tp,) + attn.shape), sd_t.reshape(n_tp, sd_rows, HD)], 1
    )
    mixed_out = lax.all_to_all(mixed_in, TP, split_axis=0, concat_axis=0, tiled=True)
    attn_all = mixed_out[:, :tok_rows]
    sd_own = mixed_out[:, tok_rows:].reshape(sd_t.shape)
    projected = jnp.einsum("tqd,tdn->qn", attn_all, ow_all, preferred_element_type=jnp.float32)
    hidden_state = resid.astype(jnp.float32) + projected
    mean_square = jnp.mean(hidden_state * hidden_state, axis=-1, keepdims=True)
    normed = (hidden_state * lax.rsqrt(mean_square + 1e-06) * norm_gain.astype(jnp.float32)).astype(
        jnp.bfloat16
    )
    own_hidden = lax.dynamic_slice_in_dim(hidden_state, tp_index * width, width, 1)
    own_normed = lax.dynamic_slice_in_dim(normed, tp_index * width, width, 1)

    logits = jnp.dot(normed, router, preferred_element_type=jnp.float32)
    expert_count = router.shape[1]
    expert_range = jnp.arange(expert_count, dtype=jnp.int32)
    picked = jnp.sum(
        jnp.where(expert_ids[:, :, None] == expert_range[None, None, :], logits[:, None, :], 0.0),
        axis=-1,
    )
    gates = jax.nn.softmax(picked, axis=-1)

    shared_gate = jnp.dot(normed, sg_w, preferred_element_type=jnp.float32)
    shared_up = jnp.dot(normed, su_w, preferred_element_type=jnp.float32)
    shared_inner = (jax.nn.silu(shared_gate) * shared_up).astype(jnp.bfloat16)

    flat_ids = expert_ids.reshape(tok_rows * TOPK)
    one_hot = (flat_ids[:, None] == expert_range[None, :]).astype(jnp.int32)
    before = jnp.cumsum(one_hot, axis=0) - one_hot
    slot = jnp.sum(one_hot * before, axis=1)
    dest = flat_ids * CAP + slot
    slots = expert_count * CAP
    place = (dest[None, :] == jnp.arange(slots, dtype=jnp.int32)[:, None]).reshape(
        slots, tok_rows, TOPK
    )
    dispatch = jnp.any(place, axis=-1).astype(jnp.bfloat16)
    buffer = jnp.dot(dispatch, own_normed, preferred_element_type=jnp.float32).astype(jnp.bfloat16)
    buffer = buffer.reshape(expert_count, CAP, width)
    recv = lax.all_to_all(buffer, SEQ, split_axis=0, concat_axis=0, tiled=True)
    ff = w_gate.shape[2]
    rows_flat = recv.reshape(slots, width)
    inner_rows = shared_inner.size // width
    carried = jnp.concatenate([rows_flat, shared_inner.reshape(inner_rows, width)], 0)
    wg_b = w_gate[0].reshape(n_tp, width, ff)
    wu_b = w_up[0].reshape(n_tp, width, ff)
    wd_b = w_down[0].reshape(n_tp, ff, w_down.shape[2])
    both = tp_gather(carried, n_tp)
    rows_all = both[:, :slots]
    sinner_all = both[:, slots:].reshape((n_tp,) + shared_inner.shape)
    shared_own = jnp.einsum("tqf,tsjf->qsj", sinner_all, sd_own, preferred_element_type=jnp.float32)
    gate_pre = jnp.einsum("tsc,tcf->sf", rows_all, wg_b, preferred_element_type=jnp.float32)
    up_pre = jnp.einsum("tsc,tcf->sf", rows_all, wu_b, preferred_element_type=jnp.float32)
    inner = (jax.nn.silu(gate_pre) * up_pre).astype(jnp.bfloat16)
    inner_all = tp_gather(inner, n_tp)
    out = jnp.einsum("tsf,tfn->sn", inner_all, wd_b, preferred_element_type=jnp.float32)
    out = out.astype(jnp.bfloat16).reshape(expert_count, CAP, w_down.shape[2])
    shared_own = shared_own.reshape(tok_rows, width)
    returned = lax.all_to_all(out, SEQ, split_axis=0, concat_axis=0, tiled=True)
    picked_rows = returned.reshape(slots, width)[dest]
    weighted = picked_rows.astype(jnp.float32) * gates.reshape(tok_rows * TOPK)[:, None]
    routed = jnp.sum(weighted.reshape(tok_rows, TOPK, width), axis=1)
    return (own_hidden + shared_own + routed).astype(jnp.bfloat16)


def solution(mesh):
    n_seq, n_tp = mesh.devices.shape
    fine = Mesh(mesh.devices.reshape(n_seq // 16, 8, 2, n_tp // 2, 2), SEQ + TP)
    return jax.shard_map(
        local,
        mesh=fine,
        in_specs=(
            P(SEQ, None),
            P(SEQ, TP),
            P(SEQ, TP),
            P(SEQ, TP),
            P(SEQ, TP),
            P(SEQ, TP),
            P(),
            P(TP, None),
            P(),
            P(),
            P(SEQ, None),
            P(SEQ, None, TP),
            P(SEQ, None, TP),
            P(SEQ, None, TP),
            P(SEQ, TP),
            P(SEQ, TP),
            P(TP, SEQ),
        ),
        out_specs=P(SEQ, TP),
        check_vma=False,
    )
```
